512 devices in a mesh: slab: 8 (over x, core), energy: 64 (over z, y).
Axes of the slice: x: 4, y: 4, z: 16, core: 2. Of those that a mesh axis runs over, the one named last changes fastest.
Arguments:
- retarded: bfloat16 [128, 3, 1536, 384], P('energy', None, 'slab'), may hold values from -0.3125 to 0.3125
- injection: bfloat16 [128, 2, 1536, 384], P('energy', None, 'slab'), may hold values from -6 to 6
- screened: bfloat16 [128, 2, 1536, 384], P('energy', None, 'slab'), may hold values from -6 to 6
- pattern: int32 [1536], P('slab'), may hold values from 0 to 1, as said below
Outputs:
- self_energy: bfloat16 [128, 2, 1536, 384], P('energy', None, 'slab')
The draws below stay inside these ranges and needn't reach their ends.
Inputs may be any that keep to these rules, and one draw needn't show every extreme that they name: `pattern`: exactly 128 of the 192 entries held by each index of slab are 1.
All inputs are finite; a program needn't handle non-finite values.
Results may differ from the reference program's by a relative error of at most 0.0058.
Values may be sent and summed in bfloat16 or wider, within the bound.
No kernel may reach another device: no remote copies, remote signals or barrier semaphores. Data moves between devices by JAX's collectives and lax.ppermute only.
A program may use at most 64 MiB of HBM per device.

```python
import math
import jax
import jax.numpy as jnp
from jax import lax

B = 192
SB = 1
ENERGIES = 128
NS = 8
ROWS = 1536
LIVE = 128


def draw_pattern(key, part):
    groups = NS // SB
    per_device = SB * B
    group_keys = jax.random.split(jax.random.fold_in(key, 17), groups)

    def one_group(group_key):
        shuffled = jax.random.permutation(group_key, per_device)
        return (shuffled < LIVE).astype(jnp.int32)
    return jax.vmap(one_group)(group_keys).reshape(NS * B)


def block_levels(stream_key, shape, cuts, least, top_value):
    factor_of, own = 1.0, jax.random.fold_in(stream_key, 6)
    for axis_at, blocks in cuts:
        draws = jnp.exp(jax.random.uniform(jax.random.fold_in(own, axis_at), (blocks,), jnp.float32, least / len(cuts), top_value / len(cuts)))
        factor_of = factor_of * jnp.repeat(draws, shape[axis_at] // blocks).reshape([-1 if axis == axis_at else 1 for axis in range(len(shape))])
    return factor_of


def centred(key, shape, scale, most, shards=(), kind=jnp.bfloat16):
    level = block_levels(key, shape, shards, -0.22, 0.18) if shards else 1.0
    entries = jax.random.normal(key, shape, jnp.float32) * scale * level
    return jnp.minimum(jnp.maximum(entries, -most), most).astype(kind)


def setup_inputs(seed: int = 0) -> dict:
    keys = jax.random.split(jax.random.key(seed), 5)
    return {
        "retarded": centred(keys[0], (ENERGIES, 3, ROWS, 2 * B), (2 * B) ** -0.5, 0.3125, ((0, 64), (2, 8))),
        "injection": centred(keys[1], (ENERGIES, 2, ROWS, 2 * B), 1.0, 6.0, ((0, 64), (2, 8))),
        "screened": centred(keys[2], (ENERGIES, 2, ROWS, 2 * B), 1.0, 6.0, ((0, 64), (2, 8))),
        "pattern": draw_pattern(jax.random.fold_in(keys[4], 71), 0),
    }


def stack_complex(blocks):
    half = blocks.shape[-1] // 2
    real_part = blocks[..., :half]
    imag_part = blocks[..., half:]
    upper = jnp.concatenate([real_part, imag_part], -1)
    lower = jnp.concatenate([-imag_part, real_part], -1)
    return jnp.concatenate([upper, lower], -2)

def convolve(green, screen):
    count = green.shape[0]
    half = green.shape[-1] // 2
    energy_index = jnp.arange(count, dtype=jnp.int32)
    phase_angle = 2.0 * math.pi / count * (energy_index[:, None] * energy_index[None, :] % count).astype(jnp.float32)
    cosine_table = jnp.cos(phase_angle)
    sine_table = jnp.sin(phase_angle)

    def transform(values):
        flat = values.reshape(count, -1)
        with_cos = jnp.dot(cosine_table, flat, precision=lax.Precision.HIGHEST).reshape(values.shape)
        with_sin = jnp.dot(sine_table, flat, precision=lax.Precision.HIGHEST).reshape(values.shape)
        return (with_cos, with_sin)

    def forward(values):
        with_cos, with_sin = transform(values.astype(jnp.float32))
        return (with_cos[..., :half] + with_sin[..., half:], with_cos[..., half:] - with_sin[..., :half])
    green_real, green_imag = forward(green)
    screen_real, screen_imag = forward(screen)
    prod_real = green_real * screen_real - green_imag * screen_imag
    prod_imag = green_real * screen_imag + green_imag * screen_real
    with_cos, with_sin = transform(jnp.concatenate([prod_real, prod_imag], -1))
    sigma_real = with_cos[..., :half] - with_sin[..., half:]
    sigma_imag = with_cos[..., half:] + with_sin[..., :half]
    factor = 1.0 / (count * math.sqrt(count))
    return jnp.concatenate([-sigma_imag, sigma_real], -1) * factor

def triple(rows_energy, inject_energy):
    zero_block = jnp.zeros((2, 1, B, 2 * B), inject_energy.dtype)
    padded = jnp.concatenate([zero_block, inject_energy, zero_block], 1)
    total = jnp.zeros((2, NS, B, 2 * B), jnp.float32)
    for offset in range(3):
        nearby = padded[:, offset:offset + NS]
        expanded = stack_complex(nearby).astype(jnp.float32)
        row_block = rows_energy[offset].astype(jnp.float32)
        left_product = jnp.einsum('nac,lncd->lnad', row_block, expanded).astype(jnp.bfloat16)
        left_product = lax.optimization_barrier(left_product)
        left_wide = left_product.astype(jnp.float32)
        swapped = jnp.concatenate([left_wide[..., B:], -left_wide[..., :B]], -1)
        real_part = jnp.einsum('lnac,nbc->lnab', left_wide, row_block)
        imag_part = jnp.einsum('lnac,nbc->lnab', swapped, row_block)
        total = total + jnp.concatenate([real_part, imag_part], -1)
    return total.astype(jnp.bfloat16)

def reference(retarded, injection, screened, pattern):
    rows_all = retarded.reshape(ENERGIES, 3, NS, B, 2 * B)
    inject_all = injection.reshape(ENERGIES, 2, NS, B, 2 * B)
    screen_all = screened.reshape(ENERGIES, 2, NS, B, 2 * B)

    def one_energy(pair):
        return triple(pair[0], pair[1])
    green = lax.map(one_energy, (rows_all, inject_all))

    def one_block(index):
        green_block = lax.dynamic_index_in_dim(green, index, 2, keepdims=False)
        screen_block = lax.dynamic_index_in_dim(screen_all, index, 2, keepdims=False)
        return convolve(green_block, screen_block)
    sigma = lax.map(one_block, jnp.arange(NS, dtype=jnp.int32))
    sigma = jnp.moveaxis(sigma, 0, 2).reshape(ENERGIES, 2, ROWS, 2 * B)
    sigma = sigma * pattern.astype(jnp.float32)[None, None, :, None]
    return sigma.astype(jnp.bfloat16)
```

```python
import math

import jax
import jax.numpy as jnp
import numpy as np
from jax import lax
from jax.experimental import pallas as pl
from jax.experimental.pallas import tpu as pltpu
from jax.sharding import PartitionSpec as P

B = 192
LIVE = 128
ENERGIES = 128
GROUPS = 64
CHUNK = 8
PACKED = GROUPS * CHUNK
F32 = jnp.float32
BF16 = jnp.bfloat16


def iota(shape, dim):
    return lax.broadcasted_iota(jnp.int32, shape, dim)


def ones_where(condition):
    return jnp.where(condition, 1.0, 0.0).astype(BF16)


def rank_row(pattern):
    live = jnp.broadcast_to(pattern, (16, B)) == 1
    upto = ones_where(iota((B, B), 0) <= iota((B, B), 1))
    count = jnp.dot(ones_where(live), upto, preferred_element_type=F32)
    return jnp.where(live, count - 1.0, -1.0).astype(jnp.int32)[:1]


def rank_column(pattern):
    live = jnp.broadcast_to(pattern, (B, 128)) == 1
    upto = ones_where(iota((B, B), 1) <= iota((B, B), 0))
    count = jnp.dot(upto, ones_where(live), preferred_element_type=F32)
    return jnp.where(live, count - 1.0, -1.0).astype(jnp.int32)[:, :1]


def pack_kernel(pattern_ref, screened_ref, out_ref):
    rank = rank_row(pattern_ref[...])
    place = iota((PACKED, 1), 0)
    wanted = (place % 2) * GROUPS + place // CHUNK
    owner = (place % CHUNK) // 2
    total = jnp.zeros((PACKED, 2 * B), F32)
    for block in range(4):
        target = jnp.where(owner == block, wanted, -2)
        select = ones_where(rank == target)
        total += jnp.dot(select, screened_ref[block], preferred_element_type=F32)
    out_ref[...] = total.astype(BF16).reshape(GROUPS, CHUNK, 2 * B)


def green_kernel(pattern_ref, retarded_ref, left_ref, own_ref, right_ref, out_ref, green_ref):
    rank = rank_row(pattern_ref[...])
    select = ones_where(rank == iota((LIVE, 1), 0))
    for energy in range(2):
        total = jnp.zeros((2 * LIVE, 2 * B), F32)
        for offset, inject_ref in enumerate((left_ref, own_ref, right_ref)):
            rows = retarded_ref[energy, offset]
            live_rows = jnp.dot(select, rows, preferred_element_type=F32).astype(BF16)
            firsts = []
            for kind in range(2):
                inject = inject_ref[energy, kind]
                lower = jnp.concatenate([-inject[:, B:], inject[:, :B]], 1)
                stacked = jnp.concatenate([inject, lower], 0)
                firsts.append(
                    jnp.dot(live_rows, stacked, preferred_element_type=F32).astype(BF16)
                )
            first = jnp.concatenate(firsts, 0)
            turned = jnp.concatenate([-rows[:, B:], rows[:, :B]], 1)
            both = jnp.concatenate([rows, turned], 0)
            total += lax.dot_general(
                first, both, (((1,), (1,)), ((), ())), preferred_element_type=F32
            )
        green_ref[energy * 2 * LIVE : (energy + 1) * 2 * LIVE, :] = total.astype(BF16)
    place = iota((PACKED, 1), 0)
    source = (place % CHUNK) * GROUPS + place // CHUNK
    order = ones_where(iota((PACKED, PACKED), 1) == source)
    packed = jnp.dot(order, green_ref[...], preferred_element_type=F32)
    out_ref[...] = packed.astype(BF16).reshape(GROUPS, CHUNK, 2 * B)


def convolve_kernel(high_ref, low_ref, green_ref, screen_ref, out_ref):
    place = iota((PACKED, 1), 0)
    energy = place % ENERGIES
    source = (energy // 2) * CHUNK + (energy % 2) * 4 + place // ENERGIES
    order = ones_where(iota((PACKED, PACKED), 1) == source)
    high, low = high_ref[...], low_ref[...]

    def ordered(ref):
        cells = ref[...].reshape(PACKED, 2 * B)
        real = jnp.dot(order, cells[:, :B], preferred_element_type=F32).astype(BF16)
        imag = jnp.dot(order, cells[:, B:], preferred_element_type=F32).astype(BF16)
        return real, imag

    def forward(real, imag, at):
        rows = slice(at * ENERGIES, (at + 1) * ENERGIES)
        stacked = jnp.concatenate([real[rows], imag[rows]], 0)
        out = jnp.dot(high, stacked, preferred_element_type=F32)
        out += jnp.dot(low, stacked, preferred_element_type=F32)
        return out[:ENERGIES], out[ENERGIES:]

    green = ordered(green_ref)
    screen = ordered(screen_ref)
    factor = 1.0 / (ENERGIES * math.sqrt(ENERGIES))
    reals, imags = [], []
    for at in range(4):
        gr, gi = forward(*green, at)
        wr, wi = forward(*screen, at)
        prod = jnp.concatenate([gr * wr - gi * wi, -(gr * wi + gi * wr)], 0)
        prod_high = prod.astype(BF16)
        prod_low = (prod - prod_high.astype(F32)).astype(BF16)
        out = jnp.dot(high, prod_high, preferred_element_type=F32)
        out += jnp.dot(high, prod_low, preferred_element_type=F32)
        out += jnp.dot(low, prod_high, preferred_element_type=F32)
        out = (out * factor).astype(BF16)
        imags.append(out[:ENERGIES])
        reals.append(out[ENERGIES:])
    place = iota((PACKED, 1), 0)
    back = (place % 4) * ENERGIES + (place // CHUNK) * 2 + (place // 4) % 2
    order = ones_where(iota((PACKED, PACKED), 1) == back)
    real = jnp.dot(order, jnp.concatenate(reals, 0), preferred_element_type=F32)
    imag = jnp.dot(order, jnp.concatenate(imags, 0), preferred_element_type=F32)
    out_ref[...] = jnp.concatenate([real, imag], 1).astype(BF16).reshape(GROUPS, CHUNK, 2 * B)


def expand_kernel(pattern_ref, packed_ref, out_ref):
    rank = rank_column(pattern_ref[...])
    place = iota((1, PACKED), 1)
    holds = (place % 2) * GROUPS + place // CHUNK
    owner = (place % CHUNK) // 2
    packed = packed_ref[...].reshape(PACKED, 2 * B)
    for block in range(4):
        select = ones_where(rank == jnp.where(owner == block, holds, -2))
        out_ref[block] = jnp.dot(select, packed, preferred_element_type=F32).astype(BF16)


def tables():
    index = np.arange(ENERGIES)
    angle = 2.0 * np.pi / ENERGIES * (index[:, None] * index[None, :] % ENERGIES)
    cosine, sine = np.cos(angle), np.sin(angle)
    whole = np.block([[cosine, sine], [-sine, cosine]]).astype(np.float32)
    high = whole.astype(BF16)
    low = (whole - high.astype(np.float32)).astype(BF16)
    return jnp.asarray(high), jnp.asarray(low)


def call(kernel, shape, *operands, scratch=()):
    return pl.pallas_call(
        kernel,
        out_shape=jax.ShapeDtypeStruct(shape, BF16),
        scratch_shapes=scratch,
        compiler_params=pltpu.CompilerParams(vmem_limit_bytes=48 << 20),
    )(*operands)


def exchange(packed):
    return lax.all_to_all(packed, "energy", split_axis=0, concat_axis=0, tiled=True)


def local(retarded, injection, screened, pattern):
    packed_shape = (GROUPS, CHUNK, 2 * B)
    row, column = pattern.reshape(1, B), pattern.reshape(B, 1)
    count = lax.axis_size("slab")
    up = [(i, i + 1) for i in range(count - 1)]
    left = lax.ppermute(injection, "slab", up)
    right = lax.ppermute(injection, "slab", [(b, a) for a, b in up])
    screen = call(pack_kernel, packed_shape, row, screened.reshape(4, B, 2 * B))
    screen = exchange(screen)
    green = call(
        green_kernel,
        packed_shape,
        row,
        retarded,
        left,
        injection,
        right,
        scratch=[pltpu.VMEM((PACKED, 2 * B), BF16)],
    )
    green = exchange(green)
    sigma = call(convolve_kernel, packed_shape, *tables(), green, screen)
    sigma = exchange(sigma)
    out = call(expand_kernel, (4, B, 2 * B), column, sigma)
    return out.reshape(2, 2, B, 2 * B)


def solution(mesh):
    placed = P("energy", None, "slab", None)
    return jax.shard_map(
        local,
        mesh=mesh,
        in_specs=(placed, placed, placed, P("slab")),
        out_specs=placed,
        check_vma=False,
    )
```

```python
import math

import jax
import jax.numpy as jnp
import numpy as np
from jax import lax
from jax.experimental import pallas as pl
from jax.experimental.pallas import tpu as pltpu
from jax.sharding import PartitionSpec as P

B = 192
LIVE = 128
ENERGIES = 128
GROUPS = 64
CHUNK = 8
PACKED = GROUPS * CHUNK
F32 = jnp.float32
BF16 = jnp.bfloat16


def iota(shape, dim):
    return lax.broadcasted_iota(jnp.int32, shape, dim)


def ones_where(condition):
    return jnp.where(condition, 1.0, 0.0).astype(BF16)


def rank_row(pattern):
    live = jnp.broadcast_to(pattern, (16, B)) == 1
    upto = ones_where(iota((B, B), 0) <= iota((B, B), 1))
    count = jnp.dot(ones_where(live), upto, preferred_element_type=F32)
    return jnp.where(live, count - 1.0, -1.0).astype(jnp.int32)[:1]


def rank_column(pattern):
    live = jnp.broadcast_to(pattern, (B, 128)) == 1
    upto = ones_where(iota((B, B), 1) <= iota((B, B), 0))
    count = jnp.dot(upto, ones_where(live), preferred_element_type=F32)
    return jnp.where(live, count - 1.0, -1.0).astype(jnp.int32)[:, :1]


def pack_kernel(spot_ref, pattern_hbm, screened_hbm, out_ref, pattern_ref, screened_ref, sems):
    copies = [pltpu.make_async_copy(pattern_hbm, pattern_ref, sems.at[4])]
    for block in range(4):
        copies.append(
            pltpu.make_async_copy(
                screened_hbm.at[block], screened_ref.at[block], sems.at[block]
            )
        )
    for copy in copies:
        copy.start()
    place = iota((PACKED, 1), 0)
    chunk = place // CHUNK
    wanted = (place % 2) * GROUPS + (chunk // 4) * 4 + (chunk + spot_ref[0]) % 4
    owner = (place % CHUNK) // 2
    copies[0].wait()
    rank = rank_row(pattern_ref[...])
    total = jnp.zeros((PACKED, 2 * B), F32)
    for block in range(4):
        select = ones_where(rank == jnp.where(owner == block, wanted, -2))
        copies[block + 1].wait()
        total += jnp.dot(select, screened_ref[block], preferred_element_type=F32)
    out_ref[...] = total.astype(BF16).reshape(16, 4 * CHUNK, 2 * B)


def turned(cells):
    return jnp.concatenate([-cells[:, B:], cells[:, :B]], 1)


def green_term(live, rows, inject_ref, energy):
    live_rows = jnp.dot(live, rows, preferred_element_type=F32).astype(BF16)
    firsts = []
    for kind in range(2):
        inject = inject_ref[energy, kind]
        stacked = jnp.concatenate([inject, turned(inject)], 0)
        firsts.append(jnp.dot(live_rows, stacked, preferred_element_type=F32).astype(BF16))
    both = jnp.concatenate([rows, turned(rows)], 0)
    return lax.dot_general(
        jnp.concatenate(firsts, 0), both, (((1,), (1,)), ((), ())), preferred_element_type=F32
    )


def near_kernel(odd_ref, pattern_ref, retarded_ref, own_ref, near_ref, total_ref, live_ref, order_ref):
    live = ones_where(rank_row(pattern_ref[...]) == iota((LIVE, 1), 0))
    live_ref[...] = live
    side = 2 - 2 * odd_ref[0]
    for energy in range(2):
        total = green_term(live, retarded_ref[energy, 1], own_ref, energy)
        total += green_term(live, retarded_ref[energy, side], near_ref, energy)
        total_ref[energy] = total
    place = iota((PACKED, 1), 0)
    source = (place % CHUNK) * GROUPS + place // CHUNK
    order_ref[...] = ones_where(iota((PACKED, PACKED), 1) == source)


def far_kernel(odd_ref, live_ref, retarded_ref, far_ref, total_ref, order_ref, out_ref):
    side = 2 * odd_ref[0]
    live = live_ref[...]
    greens = []
    for energy in range(2):
        term = green_term(live, retarded_ref[energy, side], far_ref, energy)
        greens.append((total_ref[energy] + term).astype(BF16))
    packed = jnp.dot(order_ref[...], jnp.concatenate(greens, 0), preferred_element_type=F32)
    out_ref[...] = packed.astype(BF16).reshape(GROUPS, CHUNK, 2 * B)


def ordered(order, cells):
    real = jnp.dot(order, cells[:, :B], preferred_element_type=F32).astype(BF16)
    imag = jnp.dot(order, cells[:, B:], preferred_element_type=F32).astype(BF16)
    return real, imag


def forward(high, low, real, imag, at):
    rows = slice(at * ENERGIES, (at + 1) * ENERGIES)
    stacked = jnp.concatenate([real[rows], imag[rows]], 0)
    out = jnp.dot(high, stacked, preferred_element_type=F32)
    return out + jnp.dot(low, stacked, preferred_element_type=F32)


def screen_kernel(spot_ref, high_ref, low_ref, *refs):
    screen_refs, (out_ref, order_ref, back_ref) = refs[:4], refs[4:]
    cell = iota((1, PACKED), 1)
    within = cell % ENERGIES
    origin = (within // CHUNK) * 4 + (spot_ref[0] + 4 - cell // ENERGIES) % 4
    target = (cell % 4) * ENERGIES + origin * 2 + (cell % CHUNK) // 4
    order = ones_where(iota((PACKED, PACKED), 0) == target)
    cells = [ref[...].reshape(ENERGIES, 2 * B) for ref in screen_refs]
    real, imag = ordered(order, jnp.concatenate(cells, 0))
    for at in range(4):
        out_ref[at] = forward(high_ref[...], low_ref[...], real, imag, at)
    place = iota((PACKED, 1), 0)
    energy = place % ENERGIES
    source = (energy // 2) * CHUNK + (energy % 2) * 4 + place // ENERGIES
    order_ref[...] = ones_where(iota((PACKED, PACKED), 1) == source)
    back = (place % 4) * ENERGIES + (place // CHUNK) * 2 + (place // 4) % 2
    back_ref[...] = ones_where(iota((PACKED, PACKED), 1) == back)


def convolve_kernel(high_ref, low_ref, order_ref, back_ref, screen_ref, green_ref, out_ref):
    high, low = high_ref[...], low_ref[...]
    green = ordered(order_ref[...], green_ref[...].reshape(PACKED, 2 * B))
    factor = 1.0 / (ENERGIES * math.sqrt(ENERGIES))
    reals, imags = [], []
    for at in range(4):
        out = forward(high, low, *green, at)
        gr, gi = out[:ENERGIES], out[ENERGIES:]
        wr, wi = screen_ref[at, :ENERGIES], screen_ref[at, ENERGIES:]
        prod = jnp.concatenate([gr * wr - gi * wi, -(gr * wi + gi * wr)], 0)
        prod_high = prod.astype(BF16)
        prod_low = (prod - prod_high.astype(F32)).astype(BF16)
        out = jnp.dot(high, prod_high, preferred_element_type=F32)
        out += jnp.dot(high, prod_low, preferred_element_type=F32)
        out += jnp.dot(low, prod_high, preferred_element_type=F32)
        out = (out * factor).astype(BF16)
        imags.append(out[:ENERGIES])
        reals.append(out[ENERGIES:])
    back = back_ref[...]
    real = jnp.dot(back, jnp.concatenate(reals, 0), preferred_element_type=F32)
    imag = jnp.dot(back, jnp.concatenate(imags, 0), preferred_element_type=F32)
    out_ref[...] = jnp.concatenate([real, imag], 1).astype(BF16).reshape(GROUPS, CHUNK, 2 * B)


def select_kernel(pattern_ref, out_ref):
    rank = rank_column(pattern_ref[...])
    place = iota((1, PACKED), 1)
    holds = (place % 2) * GROUPS + place // CHUNK
    owner = (place % CHUNK) // 2
    for block in range(4):
        out_ref[block] = ones_where(rank == jnp.where(owner == block, holds, -2))


def expand_kernel(select_ref, packed_ref, out_hbm, out_ref, sems):
    packed = packed_ref[...].reshape(PACKED, 2 * B)
    copies = []
    for block in range(4):
        rows = jnp.dot(select_ref[block], packed, preferred_element_type=F32)
        out_ref[block] = rows.astype(BF16)
        copies.append(
            pltpu.make_async_copy(out_ref.at[block], out_hbm.at[block], sems.at[block])
        )
        copies[-1].start()
    for copy in copies:
        copy.wait()


def tables():
    index = np.arange(ENERGIES)
    angle = 2.0 * np.pi / ENERGIES * (index[:, None] * index[None, :] % ENERGIES)
    cosine, sine = np.cos(angle), np.sin(angle)
    whole = np.block([[cosine, sine], [-sine, cosine]]).astype(np.float32)
    high = whole.astype(BF16)
    low = (whole - high.astype(np.float32)).astype(BF16)
    return jnp.asarray(high), jnp.asarray(low)


VMEM, SMEM, HBM = pltpu.VMEM, pltpu.SMEM, pltpu.HBM


def call(kernel, outs, *operands, spaces=None, out_space=VMEM, scratch=(), room=48):
    spaces = spaces or [VMEM] * len(operands)
    return pl.pallas_call(
        kernel,
        in_specs=[pl.BlockSpec(memory_space=space) for space in spaces],
        out_specs=jax.tree.map(lambda _: pl.BlockSpec(memory_space=out_space), outs),
        out_shape=outs,
        scratch_shapes=scratch,
        compiler_params=pltpu.CompilerParams(vmem_limit_bytes=room << 20),
    )(*operands)


def array(shape, kind=BF16):
    return jax.ShapeDtypeStruct(shape, kind)


def exchange(packed, groups=None):
    return lax.all_to_all(
        packed, "energy", split_axis=0, concat_axis=0, tiled=True, axis_index_groups=groups
    )


def swapped(cells, pairs):
    return lax.ppermute(cells, "slab", pairs + [(b, a) for a, b in pairs])


def local(retarded, injection, screened, pattern):
    packed = array((GROUPS, CHUNK, 2 * B))
    row, column = pattern.reshape(1, B), pattern.reshape(B, 1)
    spot = (lax.axis_index("energy") & 3).reshape(1)
    high, low = tables()
    screen = call(
        pack_kernel,
        array((16, 4 * CHUNK, 2 * B)),
        spot,
        row,
        screened.reshape(4, B, 2 * B),
        spaces=[SMEM, HBM, HBM],
        room=64,
        scratch=[
            VMEM((1, B), jnp.int32),
            VMEM((4, B, 2 * B), BF16),
            pltpu.SemaphoreType.DMA((5,)),
        ],
    )
    with jax.named_scope("screens"):
        screen = exchange(screen, [[4 * z + y for z in range(16)] for y in range(4)])
    count = lax.axis_size("slab")
    odd = (lax.axis_index("slab") & 1).reshape(1)
    with jax.named_scope("halo"):
        far = swapped(injection, [(i, i + 1) for i in range(1, count - 1, 2)])
        near = swapped(injection, [(i, i + 1) for i in range(0, count, 2)])
    total, live, order = call(
        near_kernel,
        [array((2, 2 * LIVE, 2 * B), F32), array((LIVE, B)), array((PACKED, PACKED))],
        odd,
        row,
        retarded,
        injection,
        near,
        spaces=[SMEM] + [VMEM] * 4,
    )
    green = call(
        far_kernel,
        packed,
        odd,
        live,
        retarded,
        far,
        total,
        order,
        spaces=[SMEM] + [VMEM] * 5,
    )
    with jax.named_scope("greens"):
        green = exchange(green)
    screen = screen.reshape(16, 4, CHUNK, 2 * B)
    with jax.named_scope("side"):
        screen = [screen[:, 0]] + [
            lax.ppermute(
                screen[:, step],
                "energy",
                [(4 * z + y, 4 * z + (y + step) % 4) for z in range(16) for y in range(4)],
            )
            for step in range(1, 4)
        ]
    with jax.named_scope("early"):
        screen, order, back = call(
            screen_kernel,
            [
                array((4, 2 * ENERGIES, B), F32),
                array((PACKED, PACKED)),
                array((PACKED, PACKED)),
            ],
            spot,
            high,
            low,
            *screen,
            spaces=[SMEM] + [VMEM] * 6,
        )
    sigma = call(convolve_kernel, packed, high, low, order, back, screen, green)
    with jax.named_scope("sigmas"):
        sigma = exchange(sigma)
    select = call(select_kernel, array((4, B, PACKED)), column)
    out = call(
        expand_kernel,
        array((4, B, 2 * B)),
        select,
        sigma,
        out_space=HBM,
        scratch=[VMEM((4, B, 2 * B), BF16), pltpu.SemaphoreType.DMA((4,))],
    )
    return out.reshape(2, 2, B, 2 * B)


def solution(mesh):
    placed = P("energy", None, "slab", None)
    return jax.shard_map(
        local,
        mesh=mesh,
        in_specs=(placed, placed, placed, P("slab")),
        out_specs=placed,
        check_vma=False,
    )
```

```python
import math

import jax
import jax.numpy as jnp
import numpy as np
from jax import lax
from jax.experimental import pallas as pl
from jax.experimental.pallas import tpu as pltpu
from jax.sharding import PartitionSpec as P

B = 192
LIVE = 128
ENERGIES = 128
GROUPS = 64
CHUNK = 8
PACKED = GROUPS * CHUNK
SCREEN_ROOT, GREEN_ROOT, SIGMA_ROOT = 0, 8, 8
F32 = jnp.float32
BF16 = jnp.bfloat16


def iota(shape, dim):
    return lax.broadcasted_iota(jnp.int32, shape, dim)


def ones_where(condition):
    return jnp.where(condition, 1.0, 0.0).astype(BF16)


def rank_row(pattern):
    live = jnp.broadcast_to(pattern, (16, B)) == 1
    upto = ones_where(iota((B, B), 0) <= iota((B, B), 1))
    count = jnp.dot(ones_where(live), upto, preferred_element_type=F32)
    return jnp.where(live, count - 1.0, -1.0).astype(jnp.int32)[:1]


def rank_column(pattern):
    live = jnp.broadcast_to(pattern, (B, 128)) == 1
    upto = ones_where(iota((B, B), 1) <= iota((B, B), 0))
    count = jnp.dot(upto, ones_where(live), preferred_element_type=F32)
    return jnp.where(live, count - 1.0, -1.0).astype(jnp.int32)[:, :1]


def pack_kernel(spot_ref, pattern_hbm, screened_hbm, out_ref, pattern_ref, screened_ref, sems):
    copies = [pltpu.make_async_copy(pattern_hbm, pattern_ref, sems.at[4])]
    for block in range(4):
        copies.append(
            pltpu.make_async_copy(
                screened_hbm.at[block], screened_ref.at[block], sems.at[block]
            )
        )
    for copy in copies:
        copy.start()
    place = iota((PACKED, 1), 0)
    chunk = place // CHUNK
    device = (chunk // 4 + SCREEN_ROOT) % 16 * 4 + (chunk + spot_ref[0]) % 4
    wanted = (place % 2) * GROUPS + device
    owner = (place % CHUNK) // 2
    copies[0].wait()
    rank = rank_row(pattern_ref[...])
    total = jnp.zeros((PACKED, 2 * B), F32)
    for block in range(4):
        select = ones_where(rank == jnp.where(owner == block, wanted, -2))
        copies[block + 1].wait()
        total += jnp.dot(select, screened_ref[block], preferred_element_type=F32)
    out_ref[...] = total.astype(BF16).reshape(16, 4 * CHUNK, 2 * B)


def turned(cells):
    return jnp.concatenate([-cells[:, B:], cells[:, :B]], 1)


def green_term(live, rows, inject_ref, energy):
    live_rows = jnp.dot(live, rows, preferred_element_type=F32).astype(BF16)
    firsts = []
    for kind in range(2):
        inject = inject_ref[energy, kind]
        stacked = jnp.concatenate([inject, turned(inject)], 0)
        firsts.append(jnp.dot(live_rows, stacked, preferred_element_type=F32).astype(BF16))
    both = jnp.concatenate([rows, turned(rows)], 0)
    return lax.dot_general(
        jnp.concatenate(firsts, 0), both, (((1,), (1,)), ((), ())), preferred_element_type=F32
    )


def near_kernel(odd_ref, pattern_ref, retarded_ref, own_ref, near_ref, total_ref, live_ref):
    live = ones_where(rank_row(pattern_ref[...]) == iota((LIVE, 1), 0))
    live_ref[...] = live
    side = 2 - 2 * odd_ref[0]
    for energy in range(2):
        total = green_term(live, retarded_ref[energy, 1], own_ref, energy)
        total += green_term(live, retarded_ref[energy, side], near_ref, energy)
        total_ref[energy] = total


def far_kernel(odd_ref, live_ref, retarded_ref, far_ref, total_ref, order_ref, out_ref):
    side = 2 * odd_ref[0]
    live = live_ref[...]
    greens = []
    for energy in range(2):
        term = green_term(live, retarded_ref[energy, side], far_ref, energy)
        greens.append((total_ref[energy] + term).astype(BF16))
    packed = jnp.dot(order_ref[...], jnp.concatenate(greens, 0), preferred_element_type=F32)
    out_ref[...] = packed.astype(BF16).reshape(GROUPS, CHUNK, 2 * B)


def ordered(order, cells):
    real = jnp.dot(order, cells[:, :B], preferred_element_type=F32).astype(BF16)
    imag = jnp.dot(order, cells[:, B:], preferred_element_type=F32).astype(BF16)
    return real, imag


def transform(table_ref, cells):
    out = jnp.dot(table_ref[...], cells, preferred_element_type=F32)
    return out[: 2 * ENERGIES] + out[2 * ENERGIES :]


def forward(table_ref, real, imag, at):
    rows = slice(at * ENERGIES, (at + 1) * ENERGIES)
    return transform(table_ref, jnp.concatenate([real[rows], imag[rows]], 0))


def screen_kernel(spot_ref, table_ref, *refs):
    screen_refs, (out_ref, order_ref, back_ref) = refs[:4], refs[4:]
    cell = iota((1, PACKED), 1)
    within = cell % ENERGIES
    origin = (within // CHUNK + SCREEN_ROOT) % 16 * 4 + (spot_ref[0] + 4 - cell // ENERGIES) % 4
    target = (cell % 4) * ENERGIES + origin * 2 + (cell % CHUNK) // 4
    order = ones_where(iota((PACKED, PACKED), 0) == target)
    cells = [ref[...].reshape(ENERGIES, 2 * B) for ref in screen_refs]
    real, imag = ordered(order, jnp.concatenate(cells, 0))
    for at in range(4):
        out_ref[at] = forward(table_ref, real, imag, at)
    place = iota((PACKED, 1), 0)
    energy = place % ENERGIES
    source = (energy // 2 + 64 - 4 * GREEN_ROOT) % GROUPS
    source = source * CHUNK + (energy % 2) * 4 + place // ENERGIES
    order_ref[...] = ones_where(iota((PACKED, PACKED), 1) == source)
    device = (place // CHUNK + 4 * SIGMA_ROOT) % GROUPS
    back = (place % 4) * ENERGIES + device * 2 + (place // 4) % 2
    back_ref[...] = ones_where(iota((PACKED, PACKED), 1) == back)


def convolve_kernel(table_ref, order_ref, back_ref, screen_ref, green_ref, out_ref):
    green = ordered(order_ref[...], green_ref[...].reshape(PACKED, 2 * B))
    factor = 1.0 / (ENERGIES * math.sqrt(ENERGIES))
    reals, imags = [], []
    for at in range(4):
        out = forward(table_ref, *green, at)
        gr, gi = out[:ENERGIES], out[ENERGIES:]
        wr, wi = screen_ref[at, :ENERGIES], screen_ref[at, ENERGIES:]
        prod = jnp.concatenate([gr * wr - gi * wi, -(gr * wi + gi * wr)], 0)
        prod_high = prod.astype(BF16)
        prod_low = (prod - prod_high.astype(F32)).astype(BF16)
        high = table_ref[: 2 * ENERGIES]
        out = transform(table_ref, prod_high)
        out += jnp.dot(high, prod_low, preferred_element_type=F32)
        out = (out * factor).astype(BF16)
        imags.append(out[:ENERGIES])
        reals.append(out[ENERGIES:])
    back = back_ref[...]
    real = jnp.dot(back, jnp.concatenate(reals, 0), preferred_element_type=F32)
    imag = jnp.dot(back, jnp.concatenate(imags, 0), preferred_element_type=F32)
    out_ref[...] = jnp.concatenate([real, imag], 1).astype(BF16).reshape(GROUPS, CHUNK, 2 * B)


def select_kernel(pattern_ref, out_ref):
    rank = rank_column(pattern_ref[...])
    place = iota((1, PACKED), 1)
    holds = (place % 2) * GROUPS + (place // CHUNK + 4 * SIGMA_ROOT) % GROUPS
    owner = (place % CHUNK) // 2
    for block in range(4):
        rows = slice(block * B, (block + 1) * B)
        out_ref[rows] = ones_where(rank == jnp.where(owner == block, holds, -2))


def expand_kernel(select_ref, packed_ref, out_hbm, out_ref, sems):
    packed = packed_ref[...].reshape(PACKED, 2 * B)
    rows = jnp.dot(select_ref[...], packed, preferred_element_type=F32)
    copies = []
    for block in range(4):
        out_ref[block] = rows[block * B : (block + 1) * B].astype(BF16)
        copies.append(
            pltpu.make_async_copy(out_ref.at[block], out_hbm.at[block], sems.at[block])
        )
        copies[-1].start()
    for copy in copies:
        copy.wait()


def tables():
    index = np.arange(ENERGIES)
    angle = 2.0 * np.pi / ENERGIES * (index[:, None] * index[None, :] % ENERGIES)
    cosine, sine = np.cos(angle), np.sin(angle)
    whole = np.block([[cosine, sine], [-sine, cosine]]).astype(np.float32)
    high = whole.astype(BF16)
    low = (whole - high.astype(np.float32)).astype(BF16)
    place = np.arange(PACKED)
    device = (place // CHUNK + 4 * GREEN_ROOT) % GROUPS
    order = place % CHUNK * GROUPS + device
    order = (np.arange(PACKED) == order[:, None]).astype(BF16)
    return jnp.asarray(np.concatenate([high, low], 0)), jnp.asarray(order)


VMEM, SMEM, HBM = pltpu.VMEM, pltpu.SMEM, pltpu.HBM


def call(kernel, outs, *operands, spaces=None, out_space=VMEM, scratch=(), room=48):
    spaces = spaces or [VMEM] * len(operands)
    return pl.pallas_call(
        kernel,
        in_specs=[pl.BlockSpec(memory_space=space) for space in spaces],
        out_specs=jax.tree.map(lambda _: pl.BlockSpec(memory_space=out_space), outs),
        out_shape=outs,
        scratch_shapes=scratch,
        compiler_params=pltpu.CompilerParams(vmem_limit_bytes=room << 20),
    )(*operands)


def array(shape, kind=BF16):
    return jax.ShapeDtypeStruct(shape, kind)


def along_z(root, side):
    return [(root + z) % 16 * 4 + y for z in range(16) for y in side]


def exchange(packed, groups):
    return lax.all_to_all(
        packed, "energy", split_axis=0, concat_axis=0, tiled=True, axis_index_groups=groups
    )


def swapped(cells, pairs):
    return lax.ppermute(cells, "slab", pairs + [(b, a) for a, b in pairs])


def local(retarded, injection, screened, pattern):
    packed = array((GROUPS, CHUNK, 2 * B))
    row, column = pattern.reshape(1, B), pattern.reshape(B, 1)
    spot = (lax.axis_index("energy") & 3).reshape(1)
    table, interleave = tables()
    screen = call(
        pack_kernel,
        array((16, 4 * CHUNK, 2 * B)),
        spot,
        row,
        screened.reshape(4, B, 2 * B),
        spaces=[SMEM, HBM, HBM],
        room=64,
        scratch=[
            VMEM((1, B), jnp.int32),
            VMEM((4, B, 2 * B), BF16),
            pltpu.SemaphoreType.DMA((5,)),
        ],
    )
    with jax.named_scope("screens"):
        screen = exchange(screen, [along_z(SCREEN_ROOT, (y,)) for y in range(4)])
    count = lax.axis_size("slab")
    odd = (lax.axis_index("slab") & 1).reshape(1)
    with jax.named_scope("halo"):
        far = swapped(injection, [(i, i + 1) for i in range(1, count - 1, 2)])
        near = swapped(injection, [(i, i + 1) for i in range(0, count, 2)])
    total, live = call(
        near_kernel,
        [array((2, 2 * LIVE, 2 * B), F32), array((LIVE, B))],
        odd,
        row,
        retarded,
        injection,
        near,
        spaces=[SMEM] + [VMEM] * 4,
    )
    green = call(
        far_kernel,
        packed,
        odd,
        live,
        retarded,
        far,
        total,
        interleave,
        spaces=[SMEM] + [VMEM] * 5,
    )
    with jax.named_scope("greens"):
        green = exchange(green, [along_z(GREEN_ROOT, range(4))])
    screen = screen.reshape(16, 4, CHUNK, 2 * B)
    with jax.named_scope("side"):
        screen = [screen[:, 0]] + [
            lax.ppermute(
                screen[:, step],
                "energy",
                [(4 * z + y, 4 * z + (y + step) % 4) for z in range(16) for y in range(4)],
            )
            for step in range(1, 4)
        ]
    with jax.named_scope("early"):
        screen, order, back = call(
            screen_kernel,
            [
                array((4, 2 * ENERGIES, B), F32),
                array((PACKED, PACKED)),
                array((PACKED, PACKED)),
            ],
            spot,
            table,
            *screen,
            spaces=[SMEM] + [VMEM] * 5,
        )
    sigma = call(convolve_kernel, packed, table, order, back, screen, green)
    with jax.named_scope("sigmas"):
        sigma = exchange(sigma, [along_z(SIGMA_ROOT, range(4))])
    select = call(select_kernel, array((4 * B, PACKED)), column)
    out = call(
        expand_kernel,
        array((4, B, 2 * B)),
        select,
        sigma,
        out_space=HBM,
        scratch=[VMEM((4, B, 2 * B), BF16), pltpu.SemaphoreType.DMA((4,))],
    )
    return out.reshape(2, 2, B, 2 * B)


def solution(mesh):
    placed = P("energy", None, "slab", None)
    return jax.shard_map(
        local,
        mesh=mesh,
        in_specs=(placed, placed, placed, P("slab")),
        out_specs=placed,
        check_vma=False,
    )
```

```python
import math

import jax
import jax.numpy as jnp
import numpy as np
from jax import lax
from jax.experimental import pallas as pl
from jax.experimental.pallas import tpu as pltpu
from jax.sharding import PartitionSpec as P

B = 192
LIVE = 128
ENERGIES = 128
GROUPS = 64
CHUNK = 8
PACKED = GROUPS * CHUNK
SCREEN_ORDER, GREEN_ORDER, SIGMA_ORDER = (12, False), (8, True), (8, True)
F32 = jnp.float32
BF16 = jnp.bfloat16


def iota(shape, dim):
    return lax.broadcasted_iota(jnp.int32, shape, dim)


def steps_at(slot):
    odd, half = slot % 2, slot // 2
    nonzero = (slot + 15) // 16
    return nonzero * (8 + odd * half - (1 - odd) * half)


def slot_of(steps):
    late = steps // 8
    nonzero = (steps + 15) // 16
    return nonzero * (late * (2 * steps - 15) + (1 - late) * (16 - 2 * steps))


def z_at(slot, order):
    root, far_first = order
    return (root + (steps_at(slot) if far_first else slot)) % 16


def member(z, order):
    root, far_first = order
    steps = (z + 16 - root) % 16
    return slot_of(steps) if far_first else steps


def device_at(slot, order):
    return z_at(slot // 4, order) * 4 + slot % 4


def ones_where(condition):
    return jnp.where(condition, 1.0, 0.0).astype(BF16)


def rank_row(pattern):
    live = jnp.broadcast_to(pattern, (16, B)) == 1
    upto = ones_where(iota((B, B), 0) <= iota((B, B), 1))
    count = jnp.dot(ones_where(live), upto, preferred_element_type=F32)
    return jnp.where(live, count - 1.0, -1.0).astype(jnp.int32)[:1]


def rank_column(pattern):
    live = jnp.broadcast_to(pattern, (B, 128)) == 1
    upto = ones_where(iota((B, B), 1) <= iota((B, B), 0))
    count = jnp.dot(upto, ones_where(live), preferred_element_type=F32)
    return jnp.where(live, count - 1.0, -1.0).astype(jnp.int32)[:, :1]


def pack_kernel(spot_ref, pattern_hbm, screened_hbm, out_ref, pattern_ref, screened_ref, sems):
    copies = [pltpu.make_async_copy(pattern_hbm, pattern_ref, sems.at[4])]
    for block in range(4):
        copies.append(
            pltpu.make_async_copy(
                screened_hbm.at[block], screened_ref.at[block], sems.at[block]
            )
        )
    for copy in copies:
        copy.start()
    place = iota((PACKED, 1), 0)
    chunk = place // CHUNK
    device = z_at(chunk // 4, SCREEN_ORDER) * 4 + (chunk + spot_ref[0]) % 4
    wanted = (place % 2) * GROUPS + device
    owner = (place % CHUNK) // 2
    copies[0].wait()
    rank = rank_row(pattern_ref[...])
    total = jnp.zeros((PACKED, 2 * B), F32)
    for block in range(4):
        select = ones_where(rank == jnp.where(owner == block, wanted, -2))
        copies[block + 1].wait()
        total += jnp.dot(select, screened_ref[block], preferred_element_type=F32)
    out_ref[...] = total.astype(BF16).reshape(16, 4 * CHUNK, 2 * B)


def turned(cells):
    return jnp.concatenate([-cells[:, B:], cells[:, :B]], 1)


def green_term(live, rows, inject_ref, energy):
    live_rows = jnp.dot(live, rows, preferred_element_type=F32).astype(BF16)
    firsts = []
    for kind in range(2):
        inject = inject_ref[energy, kind]
        stacked = jnp.concatenate([inject, turned(inject)], 0)
        firsts.append(jnp.dot(live_rows, stacked, preferred_element_type=F32).astype(BF16))
    both = jnp.concatenate([rows, turned(rows)], 0)
    return lax.dot_general(
        jnp.concatenate(firsts, 0), both, (((1,), (1,)), ((), ())), preferred_element_type=F32
    )


def near_kernel(odd_ref, pattern_ref, retarded_ref, own_ref, near_ref, total_ref, live_ref):
    live = ones_where(rank_row(pattern_ref[...]) == iota((LIVE, 1), 0))
    live_ref[...] = live
    side = 2 - 2 * odd_ref[0]
    for energy in range(2):
        total = green_term(live, retarded_ref[energy, 1], own_ref, energy)
        total += green_term(live, retarded_ref[energy, side], near_ref, energy)
        total_ref[energy] = total


def far_kernel(odd_ref, live_ref, retarded_ref, far_ref, total_ref, order_ref, out_ref):
    side = 2 * odd_ref[0]
    live = live_ref[...]
    greens = []
    for energy in range(2):
        term = green_term(live, retarded_ref[energy, side], far_ref, energy)
        greens.append((total_ref[energy] + term).astype(BF16))
    packed = jnp.dot(order_ref[...], jnp.concatenate(greens, 0), preferred_element_type=F32)
    out_ref[...] = packed.astype(BF16).reshape(GROUPS, CHUNK, 2 * B)


def ordered(order, cells):
    real = jnp.dot(order, cells[:, :B], preferred_element_type=F32).astype(BF16)
    imag = jnp.dot(order, cells[:, B:], preferred_element_type=F32).astype(BF16)
    return real, imag


def transform(table_ref, cells):
    out = jnp.dot(table_ref[...], cells, preferred_element_type=F32)
    return out[: 2 * ENERGIES] + out[2 * ENERGIES :]


def forward(table_ref, real, imag, at):
    rows = slice(at * ENERGIES, (at + 1) * ENERGIES)
    return transform(table_ref, jnp.concatenate([real[rows], imag[rows]], 0))


def screen_kernel(spot_ref, table_ref, *refs):
    screen_refs, (out_ref, order_ref, back_ref) = refs[:4], refs[4:]
    cell = iota((1, PACKED), 1)
    within = cell % ENERGIES
    origin = z_at(within // CHUNK, SCREEN_ORDER) * 4 + (spot_ref[0] + 4 - cell // ENERGIES) % 4
    target = (cell % 4) * ENERGIES + origin * 2 + (cell % CHUNK) // 4
    order = ones_where(iota((PACKED, PACKED), 0) == target)
    cells = [ref[...].reshape(ENERGIES, 2 * B) for ref in screen_refs]
    real, imag = ordered(order, jnp.concatenate(cells, 0))
    for at in range(4):
        out_ref[at] = forward(table_ref, real, imag, at)
    place = iota((PACKED, 1), 0)
    energy = place % ENERGIES
    source = member(energy // CHUNK, GREEN_ORDER) * 4 + energy // 2 % 4
    source = source * CHUNK + (energy % 2) * 4 + place // ENERGIES
    order_ref[...] = ones_where(iota((PACKED, PACKED), 1) == source)
    device = device_at(place // CHUNK, SIGMA_ORDER)
    back = (place % 4) * ENERGIES + device * 2 + (place // 4) % 2
    back_ref[...] = ones_where(iota((PACKED, PACKED), 1) == back)


def convolve_kernel(table_ref, order_ref, back_ref, screen_ref, green_ref, out_ref):
    green = ordered(order_ref[...], green_ref[...].reshape(PACKED, 2 * B))
    factor = 1.0 / (ENERGIES * math.sqrt(ENERGIES))
    reals, imags = [], []
    for at in range(4):
        out = forward(table_ref, *green, at)
        gr, gi = out[:ENERGIES], out[ENERGIES:]
        wr, wi = screen_ref[at, :ENERGIES], screen_ref[at, ENERGIES:]
        prod = jnp.concatenate([gr * wr - gi * wi, -(gr * wi + gi * wr)], 0)
        prod_high = prod.astype(BF16)
        prod_low = (prod - prod_high.astype(F32)).astype(BF16)
        high = table_ref[: 2 * ENERGIES]
        out = transform(table_ref, prod_high)
        out += jnp.dot(high, prod_low, preferred_element_type=F32)
        out = (out * factor).astype(BF16)
        imags.append(out[:ENERGIES])
        reals.append(out[ENERGIES:])
    back = back_ref[...]
    real = jnp.dot(back, jnp.concatenate(reals, 0), preferred_element_type=F32)
    imag = jnp.dot(back, jnp.concatenate(imags, 0), preferred_element_type=F32)
    out_ref[...] = jnp.concatenate([real, imag], 1).astype(BF16).reshape(GROUPS, CHUNK, 2 * B)


def select_kernel(pattern_ref, out_ref):
    rank = rank_column(pattern_ref[...])
    place = iota((1, PACKED), 1)
    holds = (place % 2) * GROUPS + device_at(place // CHUNK, SIGMA_ORDER)
    owner = (place % CHUNK) // 2
    for block in range(4):
        rows = slice(block * B, (block + 1) * B)
        out_ref[rows] = ones_where(rank == jnp.where(owner == block, holds, -2))


def expand_kernel(select_ref, packed_ref, out_hbm, out_ref, sems):
    packed = packed_ref[...].reshape(PACKED, 2 * B)
    rows = jnp.dot(select_ref[...], packed, preferred_element_type=F32)
    copies = []
    for block in range(4):
        out_ref[block] = rows[block * B : (block + 1) * B].astype(BF16)
        copies.append(
            pltpu.make_async_copy(out_ref.at[block], out_hbm.at[block], sems.at[block])
        )
        copies[-1].start()
    for copy in copies:
        copy.wait()


def tables():
    index = np.arange(ENERGIES)
    angle = 2.0 * np.pi / ENERGIES * (index[:, None] * index[None, :] % ENERGIES)
    cosine, sine = np.cos(angle), np.sin(angle)
    whole = np.block([[cosine, sine], [-sine, cosine]]).astype(np.float32)
    high = whole.astype(BF16)
    low = (whole - high.astype(np.float32)).astype(BF16)
    place = np.arange(PACKED)
    device = device_at(place // CHUNK, GREEN_ORDER)
    order = place % CHUNK * GROUPS + device
    order = (np.arange(PACKED) == order[:, None]).astype(BF16)
    return jnp.asarray(np.concatenate([high, low], 0)), jnp.asarray(order)


VMEM, SMEM, HBM = pltpu.VMEM, pltpu.SMEM, pltpu.HBM


def call(kernel, outs, *operands, spaces=None, out_space=VMEM, scratch=(), room=48):
    spaces = spaces or [VMEM] * len(operands)
    return pl.pallas_call(
        kernel,
        in_specs=[pl.BlockSpec(memory_space=space) for space in spaces],
        out_specs=jax.tree.map(lambda _: pl.BlockSpec(memory_space=out_space), outs),
        out_shape=outs,
        scratch_shapes=scratch,
        compiler_params=pltpu.CompilerParams(vmem_limit_bytes=room << 20),
    )(*operands)


def array(shape, kind=BF16):
    return jax.ShapeDtypeStruct(shape, kind)


def along_z(order, side):
    return [z_at(slot, order) * 4 + y for slot in range(16) for y in side]


def exchange(packed, groups):
    return lax.all_to_all(
        packed, "energy", split_axis=0, concat_axis=0, tiled=True, axis_index_groups=groups
    )


def swapped(cells, pairs):
    return lax.ppermute(cells, "slab", pairs + [(b, a) for a, b in pairs])


def local(retarded, injection, screened, pattern):
    packed = array((GROUPS, CHUNK, 2 * B))
    row, column = pattern.reshape(1, B), pattern.reshape(B, 1)
    spot = (lax.axis_index("energy") & 3).reshape(1)
    table, interleave = tables()
    screen = call(
        pack_kernel,
        array((16, 4 * CHUNK, 2 * B)),
        spot,
        row,
        screened.reshape(4, B, 2 * B),
        spaces=[SMEM, HBM, HBM],
        room=64,
        scratch=[
            VMEM((1, B), jnp.int32),
            VMEM((4, B, 2 * B), BF16),
            pltpu.SemaphoreType.DMA((5,)),
        ],
    )
    with jax.named_scope("screens"):
        screen = exchange(screen, [along_z(SCREEN_ORDER, (y,)) for y in range(4)])
    count = lax.axis_size("slab")
    odd = (lax.axis_index("slab") & 1).reshape(1)
    with jax.named_scope("halo"):
        far = swapped(injection, [(i, i + 1) for i in range(1, count - 1, 2)])
        near = swapped(injection, [(i, i + 1) for i in range(0, count, 2)])
    total, live = call(
        near_kernel,
        [array((2, 2 * LIVE, 2 * B), F32), array((LIVE, B))],
        odd,
        row,
        retarded,
        injection,
        near,
        spaces=[SMEM] + [VMEM] * 4,
    )
    green = call(
        far_kernel,
        packed,
        odd,
        live,
        retarded,
        far,
        total,
        interleave,
        spaces=[SMEM] + [VMEM] * 5,
    )
    with jax.named_scope("greens"):
        green = exchange(green, [along_z(GREEN_ORDER, range(4))])
    screen = screen.reshape(16, 4, CHUNK, 2 * B)
    with jax.named_scope("side"):
        screen = [screen[:, 0]] + [
            lax.ppermute(
                screen[:, step],
                "energy",
                [(4 * z + y, 4 * z + (y + step) % 4) for z in range(16) for y in range(4)],
            )
            for step in range(1, 4)
        ]
    with jax.named_scope("early"):
        screen, order, back = call(
            screen_kernel,
            [
                array((4, 2 * ENERGIES, B), F32),
                array((PACKED, PACKED)),
                array((PACKED, PACKED)),
            ],
            spot,
            table,
            *screen,
            spaces=[SMEM] + [VMEM] * 5,
        )
    sigma = call(convolve_kernel, packed, table, order, back, screen, green)
    with jax.named_scope("sigmas"):
        sigma = exchange(sigma, [along_z(SIGMA_ORDER, range(4))])
    select = call(select_kernel, array((4 * B, PACKED)), column)
    out = call(
        expand_kernel,
        array((4, B, 2 * B)),
        select,
        sigma,
        out_space=HBM,
        scratch=[VMEM((4, B, 2 * B), BF16), pltpu.SemaphoreType.DMA((4,))],
    )
    return out.reshape(2, 2, B, 2 * B)


def solution(mesh):
    placed = P("energy", None, "slab", None)
    return jax.shard_map(
        local,
        mesh=mesh,
        in_specs=(placed, placed, placed, P("slab")),
        out_specs=placed,
        check_vma=False,
    )
```

```python
import math

import jax
import jax.numpy as jnp
import numpy as np
from jax import lax
from jax.experimental import pallas as pl
from jax.experimental.pallas import tpu as pltpu
from jax.sharding import PartitionSpec as P

B = 192
LIVE = 128
ENERGIES = 128
GROUPS = 64
CHUNK = 8
PACKED = GROUPS * CHUNK
SCREEN_ORDER, GREEN_ORDER, SIGMA_ORDER = (12, False), (4, True), (4, True)
F32 = jnp.float32
BF16 = jnp.bfloat16


def iota(shape, dim):
    return lax.broadcasted_iota(jnp.int32, shape, dim)


def steps_at(slot):
    odd, half = slot % 2, slot // 2
    nonzero = (slot + 15) // 16
    return nonzero * (8 + odd * half - (1 - odd) * half)


def slot_of(steps):
    late = steps // 8
    nonzero = (steps + 15) // 16
    return nonzero * (late * (2 * steps - 15) + (1 - late) * (16 - 2 * steps))


def z_at(slot, order):
    root, far_first = order
    return (root + (steps_at(slot) if far_first else slot)) % 16


def member(z, order):
    root, far_first = order
    steps = (z + 16 - root) % 16
    return slot_of(steps) if far_first else steps


def device_at(slot, order):
    return z_at(slot // 4, order) * 4 + slot % 4


def ones_where(condition):
    return jnp.where(condition, 1.0, 0.0).astype(BF16)


def rank_row(pattern):
    live = jnp.broadcast_to(pattern, (16, B)) == 1
    upto = ones_where(iota((B, B), 0) <= iota((B, B), 1))
    count = jnp.dot(ones_where(live), upto, preferred_element_type=F32)
    return jnp.where(live, count - 1.0, -1.0).astype(jnp.int32)[:1]


def rank_column(pattern):
    live = jnp.broadcast_to(pattern, (B, 128)) == 1
    upto = ones_where(iota((B, B), 1) <= iota((B, B), 0))
    count = jnp.dot(upto, ones_where(live), preferred_element_type=F32)
    return jnp.where(live, count - 1.0, -1.0).astype(jnp.int32)[:, :1]


def pack_kernel(spot_ref, pattern_hbm, screened_hbm, out_ref, pattern_ref, screened_ref, sems):
    copies = [pltpu.make_async_copy(pattern_hbm, pattern_ref, sems.at[4])]
    for block in range(4):
        copies.append(
            pltpu.make_async_copy(
                screened_hbm.at[block], screened_ref.at[block], sems.at[block]
            )
        )
    for copy in copies:
        copy.start()
    place = iota((PACKED, 1), 0)
    chunk = place // CHUNK
    device = z_at(chunk // 4, SCREEN_ORDER) * 4 + (chunk + spot_ref[0]) % 4
    wanted = (place % 2) * GROUPS + device
    owner = (place % CHUNK) // 2
    copies[0].wait()
    rank = rank_row(pattern_ref[...])
    total = jnp.zeros((PACKED, 2 * B), F32)
    for block in range(4):
        select = ones_where(rank == jnp.where(owner == block, wanted, -2))
        copies[block + 1].wait()
        total += jnp.dot(select, screened_ref[block], preferred_element_type=F32)
    out_ref[...] = total.astype(BF16).reshape(16, 4 * CHUNK, 2 * B)


def turned(cells):
    return jnp.concatenate([-cells[:, B:], cells[:, :B]], 1)


def green_term(live, rows, inject_ref, energy):
    live_rows = jnp.dot(live, rows, preferred_element_type=F32).astype(BF16)
    firsts = []
    for kind in range(2):
        inject = inject_ref[energy, kind]
        stacked = jnp.concatenate([inject, turned(inject)], 0)
        firsts.append(jnp.dot(live_rows, stacked, preferred_element_type=F32).astype(BF16))
    both = jnp.concatenate([rows, turned(rows)], 0)
    return lax.dot_general(
        jnp.concatenate(firsts, 0), both, (((1,), (1,)), ((), ())), preferred_element_type=F32
    )


def near_kernel(odd_ref, pattern_ref, retarded_ref, own_ref, near_ref, total_ref, live_ref):
    live = ones_where(rank_row(pattern_ref[...]) == iota((LIVE, 1), 0))
    live_ref[...] = live
    side = 2 - 2 * odd_ref[0]
    for energy in range(2):
        total = green_term(live, retarded_ref[energy, 1], own_ref, energy)
        total += green_term(live, retarded_ref[energy, side], near_ref, energy)
        total_ref[energy] = total


def far_kernel(odd_ref, live_ref, retarded_ref, far_ref, total_ref, order_ref, out_ref):
    side = 2 * odd_ref[0]
    live = live_ref[...]
    greens = []
    for energy in range(2):
        term = green_term(live, retarded_ref[energy, side], far_ref, energy)
        greens.append((total_ref[energy] + term).astype(BF16))
    packed = jnp.dot(order_ref[...], jnp.concatenate(greens, 0), preferred_element_type=F32)
    out_ref[...] = packed.astype(BF16).reshape(GROUPS, CHUNK, 2 * B)


def ordered(order, cells):
    real = jnp.dot(order, cells[:, :B], preferred_element_type=F32).astype(BF16)
    imag = jnp.dot(order, cells[:, B:], preferred_element_type=F32).astype(BF16)
    return real, imag


def transform(table_ref, cells):
    out = jnp.dot(table_ref[...], cells, preferred_element_type=F32)
    return out[: 2 * ENERGIES] + out[2 * ENERGIES :]


def forward(table_ref, real, imag, at):
    rows = slice(at * ENERGIES, (at + 1) * ENERGIES)
    return transform(table_ref, jnp.concatenate([real[rows], imag[rows]], 0))


def screen_kernel(spot_ref, table_ref, *refs):
    screen_refs, (out_ref, order_ref, back_ref) = refs[:4], refs[4:]
    cell = iota((1, PACKED), 1)
    within = cell % ENERGIES
    origin = z_at(within // CHUNK, SCREEN_ORDER) * 4 + (spot_ref[0] + 4 - cell // ENERGIES) % 4
    target = (cell % 4) * ENERGIES + origin * 2 + (cell % CHUNK) // 4
    order = ones_where(iota((PACKED, PACKED), 0) == target)
    cells = [ref[...].reshape(ENERGIES, 2 * B) for ref in screen_refs]
    real, imag = ordered(order, jnp.concatenate(cells, 0))
    for at in range(4):
        out_ref[at] = forward(table_ref, real, imag, at)
    place = iota((PACKED, 1), 0)
    energy = place % ENERGIES
    source = member(energy // CHUNK, GREEN_ORDER) * 4 + energy // 2 % 4
    source = source * CHUNK + (energy % 2) * 4 + place // ENERGIES
    order_ref[...] = ones_where(iota((PACKED, PACKED), 1) == source)
    device = device_at(place // CHUNK, SIGMA_ORDER)
    back = (place % 4) * ENERGIES + device * 2 + (place // 4) % 2
    back_ref[...] = ones_where(iota((PACKED, PACKED), 1) == back)


def convolve_kernel(table_ref, order_ref, back_ref, screen_ref, green_ref, out_ref):
    green = ordered(order_ref[...], green_ref[...].reshape(PACKED, 2 * B))
    factor = 1.0 / (ENERGIES * math.sqrt(ENERGIES))
    reals, imags = [], []
    for at in range(4):
        out = forward(table_ref, *green, at)
        gr, gi = out[:ENERGIES], out[ENERGIES:]
        wr, wi = screen_ref[at, :ENERGIES], screen_ref[at, ENERGIES:]
        prod = jnp.concatenate([gr * wr - gi * wi, -(gr * wi + gi * wr)], 0)
        prod_high = prod.astype(BF16)
        prod_low = (prod - prod_high.astype(F32)).astype(BF16)
        high = table_ref[: 2 * ENERGIES]
        out = transform(table_ref, prod_high)
        out += jnp.dot(high, prod_low, preferred_element_type=F32)
        out = (out * factor).astype(BF16)
        imags.append(out[:ENERGIES])
        reals.append(out[ENERGIES:])
    back = back_ref[...]
    real = jnp.dot(back, jnp.concatenate(reals, 0), preferred_element_type=F32)
    imag = jnp.dot(back, jnp.concatenate(imags, 0), preferred_element_type=F32)
    out_ref[...] = jnp.concatenate([real, imag], 1).astype(BF16).reshape(GROUPS, CHUNK, 2 * B)


def select_kernel(pattern_ref, out_ref):
    rank = rank_column(pattern_ref[...])
    place = iota((1, PACKED), 1)
    holds = (place % 2) * GROUPS + device_at(place // CHUNK, SIGMA_ORDER)
    owner = (place % CHUNK) // 2
    for block in range(4):
        rows = slice(block * B, (block + 1) * B)
        out_ref[rows] = ones_where(rank == jnp.where(owner == block, holds, -2))


def expand_kernel(select_ref, packed_ref, out_hbm, out_ref, sems):
    packed = packed_ref[...].reshape(PACKED, 2 * B)
    rows = jnp.dot(select_ref[...], packed, preferred_element_type=F32)
    copies = []
    for block in range(4):
        out_ref[block] = rows[block * B : (block + 1) * B].astype(BF16)
        copies.append(
            pltpu.make_async_copy(out_ref.at[block], out_hbm.at[block], sems.at[block])
        )
        copies[-1].start()
    for copy in copies:
        copy.wait()


def tables():
    index = np.arange(ENERGIES)
    angle = 2.0 * np.pi / ENERGIES * (index[:, None] * index[None, :] % ENERGIES)
    cosine, sine = np.cos(angle), np.sin(angle)
    whole = np.block([[cosine, sine], [-sine, cosine]]).astype(np.float32)
    high = whole.astype(BF16)
    low = (whole - high.astype(np.float32)).astype(BF16)
    place = np.arange(PACKED)
    device = device_at(place // CHUNK, GREEN_ORDER)
    order = place % CHUNK * GROUPS + device
    order = (np.arange(PACKED) == order[:, None]).astype(BF16)
    return jnp.asarray(np.concatenate([high, low], 0)), jnp.asarray(order)


VMEM, SMEM, HBM = pltpu.VMEM, pltpu.SMEM, pltpu.HBM


def call(kernel, outs, *operands, spaces=None, out_space=VMEM, scratch=(), room=48):
    spaces = spaces or [VMEM] * len(operands)
    return pl.pallas_call(
        kernel,
        in_specs=[pl.BlockSpec(memory_space=space) for space in spaces],
        out_specs=jax.tree.map(lambda _: pl.BlockSpec(memory_space=out_space), outs),
        out_shape=outs,
        scratch_shapes=scratch,
        compiler_params=pltpu.CompilerParams(vmem_limit_bytes=room << 20),
    )(*operands)


def array(shape, kind=BF16):
    return jax.ShapeDtypeStruct(shape, kind)


def along_z(order, side):
    return [z_at(slot, order) * 4 + y for slot in range(16) for y in side]


def exchange(packed, groups):
    return lax.all_to_all(
        packed, "energy", split_axis=0, concat_axis=0, tiled=True, axis_index_groups=groups
    )


def swapped(cells, pairs):
    return lax.ppermute(cells, "slab", pairs + [(b, a) for a, b in pairs])


def local(retarded, injection, screened, pattern):
    packed = array((GROUPS, CHUNK, 2 * B))
    row, column = pattern.reshape(1, B), pattern.reshape(B, 1)
    spot = (lax.axis_index("energy") & 3).reshape(1)
    table, interleave = tables()
    screen = call(
        pack_kernel,
        array((16, 4 * CHUNK, 2 * B)),
        spot,
        row,
        screened.reshape(4, B, 2 * B),
        spaces=[SMEM, HBM, HBM],
        room=64,
        scratch=[
            VMEM((1, B), jnp.int32),
            VMEM((4, B, 2 * B), BF16),
            pltpu.SemaphoreType.DMA((5,)),
        ],
    )
    with jax.named_scope("screens"):
        screen = exchange(screen, [along_z(SCREEN_ORDER, (y,)) for y in range(4)])
    count = lax.axis_size("slab")
    odd = (lax.axis_index("slab") & 1).reshape(1)
    with jax.named_scope("halo"):
        far = swapped(injection, [(i, i + 1) for i in range(1, count - 1, 2)])
        near = swapped(injection, [(i, i + 1) for i in range(0, count, 2)])
    total, live = call(
        near_kernel,
        [array((2, 2 * LIVE, 2 * B), F32), array((LIVE, B))],
        odd,
        row,
        retarded,
        injection,
        near,
        spaces=[SMEM] + [VMEM] * 4,
    )
    green = call(
        far_kernel,
        packed,
        odd,
        live,
        retarded,
        far,
        total,
        interleave,
        spaces=[SMEM] + [VMEM] * 5,
    )
    with jax.named_scope("greens"):
        green = exchange(green, [along_z(GREEN_ORDER, range(4))])
    screen = screen.reshape(16, 4, CHUNK, 2 * B)
    with jax.named_scope("side"):
        screen = [screen[:, 0]] + [
            lax.ppermute(
                screen[:, step],
                "energy",
                [(4 * z + y, 4 * z + (y + step) % 4) for z in range(16) for y in range(4)],
            )
            for step in range(1, 4)
        ]
    with jax.named_scope("early"):
        screen, order, back = call(
            screen_kernel,
            [
                array((4, 2 * ENERGIES, B), F32),
                array((PACKED, PACKED)),
                array((PACKED, PACKED)),
            ],
            spot,
            table,
            *screen,
            spaces=[SMEM] + [VMEM] * 5,
        )
    sigma = call(convolve_kernel, packed, table, order, back, screen, green)
    with jax.named_scope("sigmas"):
        sigma = exchange(sigma, [along_z(SIGMA_ORDER, range(4))])
    select = call(select_kernel, array((4 * B, PACKED)), column)
    out = call(
        expand_kernel,
        array((4, B, 2 * B)),
        select,
        sigma,
        out_space=HBM,
        scratch=[VMEM((4, B, 2 * B), BF16), pltpu.SemaphoreType.DMA((4,))],
    )
    return out.reshape(2, 2, B, 2 * B)


def solution(mesh):
    placed = P("energy", None, "slab", None)
    return jax.shard_map(
        local,
        mesh=mesh,
        in_specs=(placed, placed, placed, P("slab")),
        out_specs=placed,
        check_vma=False,
    )
```
